32 devices in a mesh: gx: 4 (over y, x), gy: 8 (over z, core).
Axes of the slice: x: 2, y: 2, z: 4, core: 2. Of those that a mesh axis runs over, the one named last changes fastest.
Arguments:
- coords: float32 [3, 4, 8, 512], P(None, 'gx', 'gy'), may hold values from 0 to 16, as said below
- neighbours: int32 [4, 8, 4, 256], P('gx', 'gy'), may hold values from -1 to 4607, as said below
- noise_var: float32 [4, 8, 512], P('gx', 'gy'), may hold values from 0.05 to 0.5
- observations: float32 [4, 8, 512], P('gx', 'gy'), may hold values from -15 to 15
Outputs:
- posterior_mean: float32 [4, 8, 512], P('gx', 'gy')
- residual: float32 [4, 8, 512], P('gx', 'gy')
The draws below stay inside these ranges and needn't reach their ends.
Inputs may be any that keep to these rules, and one draw needn't show every extreme that they name: `coords`: for point p of tile (a, b) in block j = p // 128, coordinate 0 lies in [a * 2 + j // 2, a * 2 + j // 2 + 1), coordinate 1 in [b * 2 + j % 2, b * 2 + j % 2 + 1), and coordinate 2 in [0, 4). `neighbours`: each block's list names distinct points inside the grid, in the blocks of the up to eight cells that share a side or a corner with its own cell, all of which come before it in one fixed strict order of all blocks; entries -1 are empty and come after the others.
All inputs are finite; a program needn't handle non-finite values.
Results may differ from the reference program's by a relative error of at most 0.0003.
Values sent between devices are 32-bit elements; how exact they have to be, the bound alone decides.
A program may use at most 64 MiB of HBM per device.

```python
import math
import jax
import jax.numpy as jnp
from jax import lax

CELLS = 2
BLOCK = 128
NEIGH = 256
ITERS = 2
TX = 4
TY = 8
P_TILE = 512


def draw_coords(key, part):
    unit = jax.random.uniform(key, (3, TX, TY, P_TILE), jnp.float32)
    cell_of = jnp.arange(P_TILE, dtype=jnp.int32) // BLOCK
    first = (jnp.arange(TX, dtype=jnp.int32)[:, None, None] * CELLS + (cell_of // CELLS)[None, None, :]).astype(jnp.float32) + unit[0]
    second = (jnp.arange(TY, dtype=jnp.int32)[None, :, None] * CELLS + (cell_of % CELLS)[None, None, :]).astype(jnp.float32) + unit[1]
    third = 4.0 * unit[2]
    return jnp.stack([first, second, third])


def draw_neighbours(key, part):
    side_x = TX * CELLS
    side_y = TY * CELLS
    count = 8 * BLOCK
    order_key, score_key = jax.random.split(key)
    ranks = jax.random.permutation(order_key, side_x * side_y).astype(jnp.int32).reshape(side_x, side_y)
    cell_x = jnp.arange(side_x, dtype=jnp.int32)[:, None]
    cell_y = jnp.arange(side_y, dtype=jnp.int32)[None, :]
    eligible_list = []
    base_list = []
    for step_x in (-1, 0, 1):
        for step_y in (-1, 0, 1):
            if step_x == 0 and step_y == 0:
                continue
            near_x = cell_x + step_x
            near_y = cell_y + step_y
            valid = (near_x >= 0) & (near_x < side_x) & (near_y >= 0) & (near_y < side_y)
            clip_x = jnp.clip(near_x, 0, side_x - 1)
            clip_y = jnp.clip(near_y, 0, side_y - 1)
            earlier = valid & (ranks[clip_x, clip_y] < ranks)
            offset_x = clip_x // CELLS - cell_x // CELLS + 1
            offset_y = clip_y // CELLS - cell_y // CELLS + 1
            base = (offset_x * 3 + offset_y) * P_TILE + (clip_x % CELLS * CELLS + clip_y % CELLS) * BLOCK
            eligible_list.append(earlier)
            base_list.append(jnp.broadcast_to(base, (side_x, side_y)))
    eligible = jnp.stack(eligible_list, axis=2)
    bases = jnp.stack(base_list, axis=2)
    candidates = (bases[:, :, :, None] + jnp.arange(BLOCK, dtype=jnp.int32)[None, None, None, :]).reshape(side_x, side_y, count)
    allowed = jnp.broadcast_to(eligible[:, :, :, None], (side_x, side_y, 8, BLOCK)).reshape(side_x, side_y, count)
    scores = jax.random.randint(score_key, (side_x, side_y, count), 0, 65536, dtype=jnp.int32)
    keyed = (scores + allowed.astype(jnp.int32) * 131072) * count + jnp.arange(count, dtype=jnp.int32)
    top_values, top_positions = lax.top_k(keyed, NEIGH)
    chosen = jnp.take_along_axis(candidates, top_positions, axis=2)
    chosen_live = jnp.take_along_axis(allowed, top_positions, axis=2)
    result = jnp.where(chosen_live, chosen, -1).astype(jnp.int32)
    return result.reshape(TX, CELLS, TY, CELLS, NEIGH).transpose(0, 2, 1, 3, 4).reshape(TX, TY, CELLS * CELLS, NEIGH)


def draw_observations(key, part):
    across = jnp.arange(TX, dtype=jnp.float32)[:, None, None] / max(TX - 1, 1) + jnp.arange(TY, dtype=jnp.float32)[None, :, None] / max(TY - 1, 1)
    scale = 1.0 + across
    values = jnp.clip(jax.random.normal(key, (TX, TY, P_TILE), jnp.float32), -5.0, 5.0)
    return values * scale


def steps_of(rng, shape, pieces, low, largest):
    loudness = 1.0
    for axis_at, parts in pieces:
        steps = jax.random.uniform(jax.random.fold_in(jax.random.fold_in(rng, 6), axis_at), (parts,), jnp.float32, low / len(pieces), largest / len(pieces))
        loudness = loudness * jnp.repeat(jnp.exp(steps), shape[axis_at] // parts).reshape((-1,) + (1,) * (len(shape) - 1 - axis_at))
    return loudness


def setup_inputs(seed: int = 0) -> dict:
    key_list = jax.random.split(jax.random.key(seed), 5)
    coords = draw_coords(jax.random.fold_in(key_list[4], 71), 0)
    neighbours = draw_neighbours(jax.random.fold_in(key_list[4], 71), 0)
    noise_var = jnp.clip(jnp.exp(math.log(0.5) - 2.3025851 * jax.random.uniform(key_list[2], (TX, TY, P_TILE), jnp.float32) ** steps_of(key_list[2], (TX, TY, P_TILE), ((0, 4), (1, 8)), -0.2, 0.2)), 0.05, 0.5)
    observations = draw_observations(jax.random.fold_in(key_list[4], 71), 0)
    return dict(coords=coords, neighbours=neighbours, noise_var=noise_var, observations=observations)


def kernel_value(first_x, first_y, first_t, second_x, second_y, second_t):
    distance = jnp.sqrt((first_x - second_x) ** 2 + (first_y - second_y) ** 2)
    inside = jnp.maximum(1.0 - distance, 0.0)
    return inside ** 4 * (4.0 * distance + 1.0) * jnp.exp(-jnp.abs(first_t - second_t))

def block_factors(points, noise_at, live_float, block_size):
    order = points.shape[2]
    kern = kernel_value(points[:, 0, :, None], points[:, 1, :, None], points[:, 2, :, None], points[:, 0, None, :], points[:, 1, None, :], points[:, 2, None, :])
    identity = jnp.eye(order, dtype=points.dtype)
    diagonal = live_float * noise_at + (1.0 - live_float)
    covariance = kern * live_float[:, :, None] * live_float[:, None, :] + identity[None] * diagonal[:, None, :]
    lower = jnp.linalg.cholesky(covariance)
    tail = jnp.broadcast_to(identity[:, order - block_size:], (points.shape[0], order, block_size))
    solved = lax.linalg.triangular_solve(lower, tail, left_side=True, lower=True, transpose_a=True)
    return jnp.swapaxes(solved, 1, 2)

def cell_row(coord_slab, value_slab, width):
    near_coords = jnp.stack([coord_slab[:, :, shift:shift + width] for shift in range(3)], axis=2)
    near_coords = near_coords.transpose(0, 3, 1, 2, 4).reshape(3, width, -1)
    near_values = jnp.stack([value_slab[:, shift:shift + width] for shift in range(3)], axis=1)
    near_values = near_values.transpose(2, 0, 1, 3).reshape(width, -1)
    own = coord_slab[:, 1, 1:1 + width]
    kern = kernel_value(own[0][:, :, None], own[1][:, :, None], own[2][:, :, None], near_coords[0][:, None, :], near_coords[1][:, None, :], near_coords[2][:, None, :])
    return lax.optimization_barrier(jnp.sum(kern * near_values[:, None, :], axis=2))

def reference(coords, neighbours, noise_var, observations):
    tile_points = observations.shape[2]
    tile_count = TX * TY
    blocks_tile = CELLS * CELLS
    highest = lax.Precision.HIGHEST
    flat_coords = coords.reshape(3, tile_count * tile_points)
    flat_noise = noise_var.reshape(-1)
    listed = neighbours.reshape(tile_count, blocks_tile, NEIGH).astype(jnp.int32)
    listed_live = listed >= 0
    listed_safe = jnp.maximum(listed, 0).astype(jnp.int32)
    slot = listed_safe // tile_points
    within = listed_safe % tile_points
    tile_ids = jnp.arange(tile_count, dtype=jnp.int32)[:, None, None]
    tile_a = tile_ids // TY
    tile_b = tile_ids % TY
    global_ids = ((tile_a + slot // 3 - 1) * TY + tile_b + slot % 3 - 1) * tile_points + within
    global_ids = jnp.where(listed_live, global_ids, -1).astype(jnp.int32)
    own_points = jnp.arange(tile_count, dtype=jnp.int32)[:, None, None] * tile_points + jnp.arange(tile_points, dtype=jnp.int32).reshape(1, blocks_tile, BLOCK)
    index_sets = jnp.concatenate([global_ids, own_points], axis=2)
    live_sets = index_sets >= 0
    safe_sets = jnp.maximum(index_sets, 0).astype(jnp.int32)

    def precondition(vector):

        def per_tile(entry):
            safe, live = entry
            live_float = live.astype(vector.dtype)
            points = jnp.moveaxis(flat_coords[:, safe], 0, 1)
            factors = block_factors(points, flat_noise[safe], live_float, BLOCK)
            values = vector[safe] * live_float
            whitened = jnp.einsum('bij,bj->bi', factors, values, precision=highest)
            return jnp.einsum('bij,bi->bj', factors, whitened, precision=highest) * live_float
        terms = lax.map(per_tile, (safe_sets, live_sets))
        return jnp.zeros_like(vector).at[safe_sets.reshape(-1)].add(terms.reshape(-1))
    grid_coords = coords.reshape(3, TX, TY, CELLS, CELLS, BLOCK).transpose(0, 1, 3, 2, 4, 5)
    grid_coords = grid_coords.reshape(3, TX * CELLS, TY * CELLS, BLOCK)
    padded_coords = jnp.pad(grid_coords, ((0, 0), (1, 1), (1, 1), (0, 0)))
    width = TY * CELLS

    def operate(vector):
        grid_values = vector.reshape(TX, TY, CELLS, CELLS, BLOCK).transpose(0, 2, 1, 3, 4)
        grid_values = grid_values.reshape(TX * CELLS, TY * CELLS, BLOCK)
        padded_values = jnp.pad(grid_values, ((1, 1), (1, 1), (0, 0)))

        def line(position):
            coord_slab = lax.dynamic_slice_in_dim(padded_coords, position, 3, 1)
            value_slab = lax.dynamic_slice_in_dim(padded_values, position, 3, 0)
            return cell_row(coord_slab, value_slab, width)
        lines = lax.map(line, jnp.arange(TX * CELLS, dtype=jnp.int32))
        back = lines.reshape(TX, CELLS, TY, CELLS, BLOCK).transpose(0, 2, 1, 3, 4).reshape(-1)
        return back + flat_noise * vector
    flat_obs = observations.reshape(-1)
    solution = jnp.zeros_like(flat_obs)
    residual = flat_obs
    search = precondition(residual)
    direction = search
    current = jnp.sum(residual * search)
    for step in range(ITERS):
        image = operate(direction)
        alpha = current / jnp.sum(direction * image)
        solution = solution + alpha * direction
        residual = residual - alpha * image
        if step + 1 < ITERS:
            search = precondition(residual)
            following = jnp.sum(residual * search)
            direction = search + following / current * direction
            current = following
    posterior_mean = flat_obs - flat_noise * solution
    return (posterior_mean.reshape(observations.shape), residual.reshape(observations.shape))
```

```python
import functools

import jax
import jax.numpy as jnp
from jax import lax
from jax.experimental import pallas as pl
from jax.experimental.pallas import tpu as pltpu
from jax.sharding import PartitionSpec as P

MESH = pl.DeviceIdType.MESH
BLOCK = 128
NEIGH = 256
HIGH = lax.Precision.HIGHEST
DIRS = [(dx, dy) for dx in (-1, 0, 1) for dy in (-1, 0, 1) if (dx, dy) != (0, 0)]
OWN = [5, 6, 9, 10]


def around(b):
    r, c = 1 + b // 2, 1 + b % 2
    return [(r - 1 + q // 3) * 4 + c - 1 + q % 3 for q in range(9)]


def others(b):
    return [cell for q, cell in enumerate(around(b)) if q != 4]


class Links:
    def __init__(self, nx, ny):
        self.nx, self.ny = nx, ny
        self.x, self.y = lax.axis_index("gx"), lax.axis_index("gy")

    def there(self, k):
        dx, dy = DIRS[k]
        px, py = self.x + dx, self.y + dy
        return (px >= 0) & (px < self.nx) & (py >= 0) & (py < self.ny)

    def ident(self, k):
        return (self.x + DIRS[k][0], self.y + DIRS[k][1])

    def copy(self, k, slot, src, dst, send, recv):
        return pltpu.make_async_remote_copy(
            src_ref=src,
            dst_ref=dst.at[slot],
            send_sem=send.at[k],
            recv_sem=recv.at[slot],
            device_id=self.ident(k),
            device_id_type=MESH,
        )

    def start(self, src, dst, send, recv):
        for k in range(8):

            @pl.when(self.there(k))
            def _():
                self.copy(k, 7 - k, src, dst, send, recv).start()

            @pl.when(jnp.logical_not(self.there(k)))
            def _():
                dst[k] = jnp.zeros(dst.shape[1:], dst.dtype)

    def finish(self, src, dst, send, recv):
        for k in range(8):

            @pl.when(self.there(k))
            def _():
                desc = self.copy(k, k, src, dst, send, recv)
                desc.wait_send()
                desc.wait_recv()

    def greet(self, barrier, ways=range(8)):
        count = 0
        for k in ways:
            count = count + self.there(k).astype(jnp.int32)

            @pl.when(self.there(k))
            def _():
                pl.semaphore_signal(
                    barrier, inc=1, device_id=self.ident(k), device_id_type=MESH
                )

        return count


def source_of(cell):
    row, col = cell // 4 + 1, cell % 4 + 1
    dx, dy = row // 2 - 1, col // 2 - 1
    return (dx, dy), (row % 2) * 2 + col % 2


def halo_kernel(nx, ny, coords, noise, obs, out, own, land, send, recv):
    links = Links(nx, ny)
    own[...] = jnp.zeros_like(own)
    own[0:3, :] = coords[...]
    own[3:4, :] = noise[...]
    own[4:5, :] = obs[...]
    barrier = pltpu.get_barrier_semaphore()
    pl.semaphore_wait(barrier, links.greet(barrier))
    links.start(own, land, send, recv)
    links.finish(own, land, send, recv)
    for cell in range(16):
        way, inner = source_of(cell)
        part = slice(inner * BLOCK, (inner + 1) * BLOCK)
        value = own[:, part] if way == (0, 0) else land[DIRS.index(way), :, part]
        out[:, cell * BLOCK : (cell + 1) * BLOCK] = value


def kernel_value(ax, ay, at, bx, by, bt):
    dx, dy = ax - bx, ay - by
    distance = jnp.sqrt(dx * dx + dy * dy)
    inside = jnp.maximum(1.0 - distance, 0.0)
    square = inside * inside
    return square * square * (4.0 * distance + 1.0) * jnp.exp(-jnp.abs(at - bt))


def thirds(x):
    high = x.astype(jnp.bfloat16).astype(jnp.float32)
    rest = x - high
    mid = rest.astype(jnp.bfloat16).astype(jnp.float32)
    return high, mid, rest - mid


def dot(a, b, rhs=0):
    return lax.dot_general(
        a, b, (((1,), (rhs,)), ((), ())), precision=HIGH, preferred_element_type=jnp.float32
    )


def pick(a, b, rhs=0):
    return lax.dot_general(
        a, b, (((1,), (rhs,)), ((), ())), preferred_element_type=jnp.float32
    )


def iota(shape, axis):
    return lax.broadcasted_iota(jnp.int32, shape, axis)


def invert(a_ref, count):
    rows, lanes = iota((BLOCK, 1), 0), iota((1, BLOCK), 1)

    def turn(_, carry):
        mats = [a_ref[b] for b in range(count)]
        for j in range(8):
            at_row = (rows == j).astype(jnp.float32)
            at_lane = (lanes == j).astype(jnp.float32)
            for b in range(count):
                a = mats[b]
                scaled = (a[j : j + 1, :] + at_lane) * (1.0 / a[j : j + 1, j : j + 1])
                mats[b] = a - (a[:, j : j + 1] - at_row) * scaled
        for b in range(count):
            a = pltpu.roll(mats[b], BLOCK - 8, axis=1)
            a_ref[b, 0 : BLOCK - 8, :] = a[8:, :]
            a_ref[b, BLOCK - 8 :, :] = a[:8, :]
        return carry

    lax.fori_loop(0, BLOCK // 8, turn, 0)


def factor_kernel(f_ref, idx_ref, m_ref, n_ref, k_ref, a_ref, hot, c11, c21, c22, w2, w3):
    count = 4
    idx = idx_ref[...].astype(jnp.float32)
    idx_t = idx.T
    lane = iota((1, BLOCK), 1).astype(jnp.float32)
    for b in range(count):
        chosen = idx_t[:, b : b + 1]
        for q, cell in enumerate(others(b)):
            same = chosen == lane + float(cell * BLOCK)
            hot[b, :, q * BLOCK : (q + 1) * BLOCK] = same.astype(jnp.float32).astype(jnp.bfloat16)
        near = jnp.concatenate(
            [f_ref[:, cell * BLOCK : (cell + 1) * BLOCK] for cell in others(b)], axis=1
        )
        stacked = jnp.concatenate([*thirds(near), jnp.zeros_like(near)], axis=0)
        found = pick(stacked.astype(jnp.bfloat16), hot[b], 1)
        x = found[0:8] + found[8:16] + found[16:24]
        xt = x.T
        live_row = (idx[b : b + 1, :] >= 0.0).astype(jnp.float32)
        live_col = (chosen >= 0.0).astype(jnp.float32)
        diagonal = live_row * x[3:4] + (1.0 - live_row)
        on_diagonal = iota((NEIGH, NEIGH), 0) == iota((NEIGH, NEIGH), 1)
        kern = kernel_value(xt[:, 0:1], xt[:, 1:2], xt[:, 2:3], x[0:1], x[1:2], x[2:3])
        c11[b] = kern * live_col * live_row + jnp.where(on_diagonal, diagonal, 0.0)
        home = OWN[b] * BLOCK
        o = f_ref[:, home : home + BLOCK]
        ot = o.T
        kern = kernel_value(ot[:, 0:1], ot[:, 1:2], ot[:, 2:3], x[0:1], x[1:2], x[2:3])
        c21[b] = kern * live_row
        for q, cell in enumerate(around(b)):
            p = f_ref[:, cell * BLOCK : (cell + 1) * BLOCK]
            pt = p.T
            kern = kernel_value(pt[:, 0:1], pt[:, 1:2], pt[:, 2:3], o[0:1], o[1:2], o[2:3])
            k_ref[b, q * BLOCK : (q + 1) * BLOCK, :] = kern
            if q == 4:
                on_diagonal = iota((BLOCK, BLOCK), 0) == iota((BLOCK, BLOCK), 1)
                c22[b] = kern + jnp.where(on_diagonal, o[3:4], 0.0)
        a_ref[b] = c11[b, 0:BLOCK, 0:BLOCK]
    invert(a_ref, count)
    for b in range(count):
        inverse = a_ref[b]
        a21 = c11[b, BLOCK:, 0:BLOCK]
        own1 = c21[b, :, 0:BLOCK]
        left2, left3 = dot(a21, inverse), dot(own1, inverse)
        w2[b], w3[b] = left2, left3
        a_ref[b] = c11[b, BLOCK:, BLOCK:] - dot(left2, a21, 1)
        c21[b, :, BLOCK:] = c21[b, :, BLOCK:] - dot(left3, a21, 1)
        c22[b] = c22[b] - dot(left3, own1, 1)
    invert(a_ref, count)
    for b in range(count):
        own2 = c21[b, :, BLOCK:]
        b2 = dot(own2, a_ref[b])
        c21[b, :, 0:BLOCK] = dot(b2, w2[b]) - w3[b]
        a_ref[b] = c22[b] - dot(b2, own2, 1)
        c21[b, :, BLOCK:] = -b2
    invert(a_ref, count)
    eye = (iota((BLOCK, BLOCK), 0) == iota((BLOCK, BLOCK), 1)).astype(jnp.float32)
    for b in range(count):
        inverse = a_ref[b]
        compact = c21[b]
        for ref, mine, theirs in ((m_ref, eye, compact), (n_ref, inverse, dot(inverse, compact))):
            stacked = jnp.concatenate(thirds(theirs), axis=0).astype(jnp.bfloat16)
            wide = pick(stacked, hot[b])
            wide = wide[0:BLOCK] + wide[BLOCK : 2 * BLOCK] + wide[2 * BLOCK :]
            ref[b, :, 0 : 4 * BLOCK] = wide[:, : 4 * BLOCK]
            ref[b, :, 4 * BLOCK : 5 * BLOCK] = mine
            ref[b, :, 5 * BLOCK :] = wide[:, 4 * BLOCK :]


def solve_kernel(nx, ny, f_ref, m_ref, n_ref, k_ref, mean_ref, res_ref, *scratch):
    (res, terms, terms_in, total, image, image_in, sums, sums_y, sums_x) = scratch[:9]
    (send_t, recv_t, send_i, recv_i, send_y, recv_y, send_x, recv_x) = scratch[9:]
    links = Links(nx, ny)
    gx, gy = links.x, links.y
    barrier = pltpu.get_barrier_semaphore()
    corners = links.greet(barrier, [k for k in range(8) if 0 not in DIRS[k]])
    line_y = [(gx, lax.rem(gy + off, ny)) for off in range(1, ny)]
    line_x = [(lax.rem(gx + off, nx), gy) for off in range(1, nx)]
    for peer in line_y + line_x:
        pl.semaphore_signal(barrier, inc=1, device_id=peer, device_id_type=MESH)
    for cell in range(16):
        res[cell : cell + 1, :] = f_ref[4:5, cell * BLOCK : (cell + 1) * BLOCK]
    noise = [f_ref[3:4, c * BLOCK : (c + 1) * BLOCK] for c in OWN]

    def precondition(step):
        out = [jnp.zeros((1, BLOCK), jnp.float32) for _ in range(16)]
        for b in range(4):
            acc = jnp.zeros((BLOCK, BLOCK), jnp.float32)
            for q, cell in enumerate(around(b)):
                acc = acc + m_ref[b, :, q * BLOCK : (q + 1) * BLOCK] * res[cell : cell + 1, :]
            w = jnp.sum(acc, axis=1, keepdims=True)
            for q, cell in enumerate(around(b)):
                part = n_ref[b, :, q * BLOCK : (q + 1) * BLOCK] * w
                out[cell] = out[cell] + jnp.sum(part, axis=0, keepdims=True)
        for cell in range(16):
            terms[step, cell : cell + 1, :] = out[cell]

    def exchange_terms(step):
        args = (terms.at[step], terms_in.at[step], send_t.at[step], recv_t.at[step])
        links.start(*args)
        links.finish(*args)
        for cell in range(16):
            r, c = cell // 4, cell % 4
            value = terms[step, cell : cell + 1, :]
            for k, (dx, dy) in enumerate(DIRS):
                rr, cc = r - 2 * dx, c - 2 * dy
                if 0 <= rr < 4 and 0 <= cc < 4:
                    at = rr * 4 + cc
                    value = value + terms_in[step, k, at : at + 1, :]
            total[step, cell : cell + 1, :] = value

    def operate(step):
        columns = total[step].T
        for b in range(4):
            acc = jnp.zeros((BLOCK, BLOCK), jnp.float32)
            for q, cell in enumerate(around(b)):
                acc = acc + k_ref[b, q * BLOCK : (q + 1) * BLOCK, :] * columns[:, cell : cell + 1]
            value = jnp.sum(acc, axis=0, keepdims=True)
            value = value + noise[b] * total[step, OWN[b] : OWN[b] + 1, :]
            image[step, b : b + 1, :] = value

    def line_copy(step, buf, send, recv, peer, at, off):
        return pltpu.make_async_remote_copy(
            src_ref=sums.at[step, 0] if buf is sums_y else sums.at[step, 1],
            dst_ref=buf.at[step, at],
            send_sem=send.at[step, off],
            recv_sem=recv.at[step, off],
            device_id=peer,
            device_id_type=MESH,
        )

    def reduce_line(step, buf, send, recv, peers, me, size):
        copies = [line_copy(step, buf, send, recv, p, me, o) for o, p in enumerate(peers)]
        for copy in copies:
            copy.start()
        buf[step, me] = sums[step, 0] if buf is sums_y else sums[step, 1]
        for copy in copies:
            copy.wait()
        value = buf[step, 0]
        for at in range(1, size):
            value = value + buf[step, at]
        return value

    def reduce_all(step, *rows):
        sums[step, 0] = jnp.zeros((8, BLOCK), jnp.float32)
        for at, row in enumerate(rows):
            sums[step, 0, at : at + 1, :] = row
        sums[step, 1] = reduce_line(step, sums_y, send_y, recv_y, line_y, gy, ny)
        value = reduce_line(step, sums_x, send_x, recv_x, line_x, gx, nx)
        value = jnp.sum(value, axis=1, keepdims=True)
        return [value[at : at + 1, :] for at in range(len(rows))]

    def across(pairs):
        value = pairs[0][0] * pairs[0][1]
        for a, b in pairs[1:]:
            value = value + a * b
        return value

    def mine(ref, step):
        return [ref[step, c : c + 1, :] for c in OWN]

    precondition(0)
    pl.semaphore_wait(barrier, corners + nx + ny - 2)
    exchange_terms(0)
    image[...] = jnp.zeros_like(image)
    operate(0)
    args = (image.at[0], image_in, send_i, recv_i)
    links.start(*args)
    first = mine(total, 0)
    along = [image[0, b : b + 1, :] for b in range(4)]
    start = [res[c : c + 1, :] for c in OWN]
    current, curve = reduce_all(
        0, across(list(zip(start, first))), across(list(zip(first, along)))
    )
    links.finish(*args)
    alpha = current / curve
    for cell in range(16):
        way, inner = source_of(cell)
        if way == (0, 0):
            value = image[0, inner : inner + 1, :]
        else:
            value = image_in[DIRS.index(way), inner : inner + 1, :]
        res[cell : cell + 1, :] = res[cell : cell + 1, :] - alpha * value
    precondition(1)
    exchange_terms(1)
    operate(1)
    second = mine(total, 1)
    along2 = [image[1, b : b + 1, :] for b in range(4)]
    left = [res[c : c + 1, :] for c in OWN]
    following, own_curve, cross = reduce_all(
        1,
        across(list(zip(left, second))),
        across(list(zip(second, along2))),
        across(list(zip(second, along))),
    )
    ratio = following / current
    alpha2 = following / (own_curve + ratio * (2.0 * cross + ratio * curve))
    for b in range(4):
        solved = alpha * first[b] + alpha2 * (second[b] + ratio * first[b])
        mean_ref[b : b + 1, :] = start[b] - noise[b] * solved
        res_ref[b : b + 1, :] = left[b] - alpha2 * (along2[b] + ratio * along[b])


def local(nx, ny, coords, neighbours, noise_var, observations):
    tile = observations.shape[2]
    f32 = jnp.float32
    vmem = pl.BlockSpec(memory_space=pltpu.VMEM)
    dma = pltpu.SemaphoreType.DMA
    listed = neighbours.reshape(4, NEIGH)
    slot, within = listed // tile, listed % tile
    row = (slot // 3) * 2 + within // (2 * BLOCK) - 1
    col = (slot % 3) * 2 + (within // BLOCK) % 2 - 1
    index = jnp.where(listed >= 0, (row * 4 + col) * BLOCK + within % BLOCK, -1)
    index = jnp.pad(index, ((0, 4), (0, 0)))
    patch = pl.pallas_call(
        functools.partial(halo_kernel, nx, ny),
        out_shape=jax.ShapeDtypeStruct((8, 16 * BLOCK), f32),
        in_specs=[vmem] * 3,
        out_specs=vmem,
        scratch_shapes=[
            pltpu.VMEM((8, tile), f32),
            pltpu.VMEM((8, 8, tile), f32),
            dma((8,)),
            dma((8,)),
        ],
        compiler_params=pltpu.CompilerParams(collective_id=0, has_side_effects=True),
        name="halo",
    )(coords.reshape(3, tile), noise_var.reshape(1, tile), observations.reshape(1, tile))
    wide = jax.ShapeDtypeStruct((4, BLOCK, 9 * BLOCK), f32)
    square = pltpu.VMEM((4, BLOCK, BLOCK), f32)
    m, n, k = pl.pallas_call(
        factor_kernel,
        out_shape=(wide, wide, jax.ShapeDtypeStruct((4, 9 * BLOCK, BLOCK), f32)),
        in_specs=[vmem] * 2,
        out_specs=[vmem] * 3,
        scratch_shapes=[
            square,
            pltpu.VMEM((4, NEIGH, 8 * BLOCK), jnp.bfloat16),
            pltpu.VMEM((4, NEIGH, NEIGH), f32),
            pltpu.VMEM((4, BLOCK, NEIGH), f32),
            square,
            square,
            square,
        ],
        compiler_params=pltpu.CompilerParams(vmem_limit_bytes=48 << 20),
        name="factor",
    )(patch, index)
    mean, residual = pl.pallas_call(
        functools.partial(solve_kernel, nx, ny),
        out_shape=(jax.ShapeDtypeStruct((4, BLOCK), f32),) * 2,
        in_specs=[vmem] * 4,
        out_specs=[vmem] * 2,
        scratch_shapes=[
            pltpu.VMEM((16, BLOCK), f32),
            pltpu.VMEM((2, 16, BLOCK), f32),
            pltpu.VMEM((2, 8, 16, BLOCK), f32),
            pltpu.VMEM((2, 16, BLOCK), f32),
            pltpu.VMEM((2, 8, BLOCK), f32),
            pltpu.VMEM((8, 8, BLOCK), f32),
            pltpu.VMEM((2, 2, 8, BLOCK), f32),
            pltpu.VMEM((2, ny, 8, BLOCK), f32),
            pltpu.VMEM((2, nx, 8, BLOCK), f32),
            dma((2, 8)),
            dma((2, 8)),
            dma((8,)),
            dma((8,)),
            dma((2, ny)),
            dma((2, ny)),
            dma((2, nx)),
            dma((2, nx)),
        ],
        compiler_params=pltpu.CompilerParams(
            collective_id=1, has_side_effects=True, vmem_limit_bytes=48 << 20
        ),
        name="solve",
    )(patch, m, n, k)
    return (mean.reshape(observations.shape), residual.reshape(observations.shape))


def solution(mesh):
    in_specs = (
        P(None, "gx", "gy", None),
        P("gx", "gy", None, None),
        P("gx", "gy", None),
        P("gx", "gy", None),
    )
    out_specs = (P("gx", "gy", None), P("gx", "gy", None))
    body = functools.partial(local, mesh.shape["gx"], mesh.shape["gy"])
    return jax.shard_map(body, mesh=mesh, in_specs=in_specs, out_specs=out_specs, check_vma=False)
```

```python
import functools

import jax
import jax.numpy as jnp
from jax import lax
from jax.experimental import pallas as pl
from jax.experimental.pallas import tpu as pltpu
from jax.sharding import PartitionSpec as P

MESH = pl.DeviceIdType.MESH
BLOCK = 128
NEIGH = 256
HIGH = lax.Precision.HIGHEST
DIRS = [(dx, dy) for dx in (-1, 0, 1) for dy in (-1, 0, 1) if (dx, dy) != (0, 0)]
OWN = [5, 6, 9, 10]


def around(b):
    r, c = 1 + b // 2, 1 + b % 2
    return [(r - 1 + q // 3) * 4 + c - 1 + q % 3 for q in range(9)]


def others(b):
    return [cell for q, cell in enumerate(around(b)) if q != 4]


class Links:
    def __init__(self, nx, ny):
        self.nx, self.ny = nx, ny
        self.x, self.y = lax.axis_index("gx"), lax.axis_index("gy")

    def there(self, k):
        dx, dy = DIRS[k]
        px, py = self.x + dx, self.y + dy
        return (px >= 0) & (px < self.nx) & (py >= 0) & (py < self.ny)

    def ident(self, k):
        return (self.x + DIRS[k][0], self.y + DIRS[k][1])

    def copy(self, k, slot, src, dst, send, recv):
        return pltpu.make_async_remote_copy(
            src_ref=src,
            dst_ref=dst.at[slot],
            send_sem=send.at[k],
            recv_sem=recv.at[slot],
            device_id=self.ident(k),
            device_id_type=MESH,
        )

    def start(self, src, dst, send, recv):
        for k in range(8):

            @pl.when(self.there(k))
            def _():
                self.copy(k, 7 - k, src, dst, send, recv).start()

            @pl.when(jnp.logical_not(self.there(k)))
            def _():
                dst[k] = jnp.zeros(dst.shape[1:], dst.dtype)

    def finish(self, src, dst, send, recv):
        for k in range(8):

            @pl.when(self.there(k))
            def _():
                desc = self.copy(k, k, src, dst, send, recv)
                desc.wait_send()
                desc.wait_recv()

    def greet(self, barrier, ways=range(8)):
        count = 0
        for k in ways:
            count = count + self.there(k).astype(jnp.int32)

            @pl.when(self.there(k))
            def _():
                pl.semaphore_signal(
                    barrier, inc=1, device_id=self.ident(k), device_id_type=MESH
                )

        return count


def source_of(cell):
    row, col = cell // 4 + 1, cell % 4 + 1
    dx, dy = row // 2 - 1, col // 2 - 1
    return (dx, dy), (row % 2) * 2 + col % 2


def halo_kernel(nx, ny, coords, noise, obs, out, own, land, send, recv):
    links = Links(nx, ny)
    own[...] = jnp.zeros_like(own)
    own[0:3, :] = coords[...]
    own[3:4, :] = noise[...]
    own[4:5, :] = obs[...]
    barrier = pltpu.get_barrier_semaphore()
    pl.semaphore_wait(barrier, links.greet(barrier))
    links.start(own, land, send, recv)
    links.finish(own, land, send, recv)
    for cell in range(16):
        way, inner = source_of(cell)
        part = slice(inner * BLOCK, (inner + 1) * BLOCK)
        value = own[:, part] if way == (0, 0) else land[DIRS.index(way), :, part]
        out[:, cell * BLOCK : (cell + 1) * BLOCK] = value


def kernel_value(ax, ay, at, bx, by, bt):
    dx, dy = ax - bx, ay - by
    distance = jnp.sqrt(dx * dx + dy * dy)
    inside = jnp.maximum(1.0 - distance, 0.0)
    square = inside * inside
    return square * square * (4.0 * distance + 1.0) * jnp.exp(-jnp.abs(at - bt))


def thirds(x):
    high = x.astype(jnp.bfloat16).astype(jnp.float32)
    rest = x - high
    mid = rest.astype(jnp.bfloat16).astype(jnp.float32)
    return high, mid, rest - mid


def dot(a, b, rhs=0):
    return lax.dot_general(
        a, b, (((1,), (rhs,)), ((), ())), precision=HIGH, preferred_element_type=jnp.float32
    )


def pick(a, b, rhs=0):
    return lax.dot_general(
        a, b, (((1,), (rhs,)), ((), ())), preferred_element_type=jnp.float32
    )


def iota(shape, axis):
    return lax.broadcasted_iota(jnp.int32, shape, axis)


def invert(a_ref, count, mix):
    f32 = jnp.float32
    lanes = iota((1, BLOCK), 1)
    keep = lanes >= 8

    def shift(x):
        return pltpu.roll(x, BLOCK - 8, axis=1)

    def panel(p, base):
        d = [
            [jnp.broadcast_to(p[i][:, base + j : base + j + 1], (8, BLOCK)) for j in range(i + 1)]
            for i in range(8)
        ]
        if base:
            p = [shift(x) for x in p]
        y = [jnp.where(keep, p[i], (lanes == i).astype(f32)) for i in range(8)]
        low = [[None] * 8 for _ in range(8)]
        inverse = [None] * 8
        for j in range(8):
            inverse[j] = 1.0 / d[j][j]
            for i in range(j + 1, 8):
                low[i][j] = d[i][j] * inverse[j]
            for i in range(j + 1, 8):
                for k in range(j + 1, i + 1):
                    d[i][k] = d[i][k] - low[i][j] * d[k][j]
            for i in range(j + 1, 8):
                y[i] = y[i] - low[i][j] * y[j]
        u = [y[j] * inverse[j] for j in range(8)]
        for j in range(7, 0, -1):
            for i in range(j):
                u[i] = u[i] - low[j][i] * u[j]
        return u

    def advance(rows, u):
        out = []
        for row in rows:
            t = [row[:, k : k + 1] * u[k] for k in range(8)]
            total = ((t[0] + t[1]) + (t[2] + t[3])) + ((t[4] + t[5]) + (t[6] + t[7]))
            out.append(jnp.where(keep, row, 0.0) - total)
        return out

    def pack(place, b, tile):
        mix[pl.ds(place * 64 + b, 8, stride=8), :] = tile

    def unpack(place, b):
        return mix[pl.ds(place * 64 + b, 8, stride=8), :]

    def load(place):
        return [mix[place * 64 + i * 8 : place * 64 + (i + 1) * 8, :] for i in range(8)]

    def save(place, u):
        for i in range(8):
            mix[place * 64 + i * 8 : place * 64 + (i + 1) * 8, :] = u[i]

    def rest(first):
        for b in range(count):
            u = shift(unpack(3, b))
            old = a_ref[b, first * 8 :, :]
            new = shift(jnp.where(keep, old, 0.0)) - dot(old[:, 0:8], u)
            a_ref[b, first * 8 - 8 : BLOCK - 8, :] = new
            a_ref[b, BLOCK - 8 :, :] = u
            pack(2, b, new[0:8])

    for place in range(3):
        for b in range(8):
            pack(place, b, a_ref[b % count, place * 8 : place * 8 + 8, :])
    u = panel(load(0), 0)
    n = advance(load(1), u)
    save(3, u)

    def turn(_, carry):
        n, before = carry[:8], carry[8:]
        q = [shift(x) for x in advance(load(2), before)]
        u = panel(n, 8)
        rest(3)
        n = advance(q, u)
        save(3, u)
        return tuple(n) + tuple(u)

    carry = lax.fori_loop(0, BLOCK // 8 - 1, turn, tuple(n) + tuple(u))
    rest(2)
    save(0, [shift(x) for x in carry[:8]])
    for b in range(count):
        a_ref[b, 0:8, :] = unpack(0, b)


def factor_kernel(f_ref, idx_ref, m_ref, n_ref, k_ref, a_ref, hot, c11, c21, c22, w2, w3, *room):
    count = 4
    idx = idx_ref[...].astype(jnp.float32)
    idx_t = idx.T
    lane = iota((1, BLOCK), 1).astype(jnp.float32)
    for b in range(count):
        chosen = idx_t[:, b : b + 1]
        for q, cell in enumerate(others(b)):
            same = chosen == lane + float(cell * BLOCK)
            hot[b, :, q * BLOCK : (q + 1) * BLOCK] = same.astype(jnp.float32).astype(jnp.bfloat16)
        near = jnp.concatenate(
            [f_ref[:, cell * BLOCK : (cell + 1) * BLOCK] for cell in others(b)], axis=1
        )
        stacked = jnp.concatenate([*thirds(near), jnp.zeros_like(near)], axis=0)
        found = pick(stacked.astype(jnp.bfloat16), hot[b], 1)
        x = found[0:8] + found[8:16] + found[16:24]
        xt = x.T
        live_row = (idx[b : b + 1, :] >= 0.0).astype(jnp.float32)
        live_col = (chosen >= 0.0).astype(jnp.float32)
        diagonal = live_row * x[3:4] + (1.0 - live_row)
        on_diagonal = iota((NEIGH, NEIGH), 0) == iota((NEIGH, NEIGH), 1)
        kern = kernel_value(xt[:, 0:1], xt[:, 1:2], xt[:, 2:3], x[0:1], x[1:2], x[2:3])
        c11[b] = kern * live_col * live_row + jnp.where(on_diagonal, diagonal, 0.0)
        home = OWN[b] * BLOCK
        o = f_ref[:, home : home + BLOCK]
        ot = o.T
        kern = kernel_value(ot[:, 0:1], ot[:, 1:2], ot[:, 2:3], x[0:1], x[1:2], x[2:3])
        c21[b] = kern * live_row
        for q, cell in enumerate(around(b)):
            p = f_ref[:, cell * BLOCK : (cell + 1) * BLOCK]
            pt = p.T
            kern = kernel_value(pt[:, 0:1], pt[:, 1:2], pt[:, 2:3], o[0:1], o[1:2], o[2:3])
            k_ref[b, q * BLOCK : (q + 1) * BLOCK, :] = kern
            if q == 4:
                on_diagonal = iota((BLOCK, BLOCK), 0) == iota((BLOCK, BLOCK), 1)
                c22[b] = kern + jnp.where(on_diagonal, o[3:4], 0.0)
        a_ref[b] = c11[b, 0:BLOCK, 0:BLOCK]
    invert(a_ref, count, *room)
    for b in range(count):
        inverse = a_ref[b]
        a21 = c11[b, BLOCK:, 0:BLOCK]
        own1 = c21[b, :, 0:BLOCK]
        left2, left3 = dot(a21, inverse), dot(own1, inverse)
        w2[b], w3[b] = left2, left3
        a_ref[b] = c11[b, BLOCK:, BLOCK:] - dot(left2, a21, 1)
        c21[b, :, BLOCK:] = c21[b, :, BLOCK:] - dot(left3, a21, 1)
        c22[b] = c22[b] - dot(left3, own1, 1)
    invert(a_ref, count, *room)
    for b in range(count):
        own2 = c21[b, :, BLOCK:]
        b2 = dot(own2, a_ref[b])
        c21[b, :, 0:BLOCK] = dot(b2, w2[b]) - w3[b]
        a_ref[b] = c22[b] - dot(b2, own2, 1)
        c21[b, :, BLOCK:] = -b2
    invert(a_ref, count, *room)
    eye = (iota((BLOCK, BLOCK), 0) == iota((BLOCK, BLOCK), 1)).astype(jnp.float32)
    for b in range(count):
        inverse = a_ref[b]
        compact = c21[b]
        for ref, mine, theirs in ((m_ref, eye, compact), (n_ref, inverse, dot(inverse, compact))):
            stacked = jnp.concatenate(thirds(theirs), axis=0).astype(jnp.bfloat16)
            wide = pick(stacked, hot[b])
            wide = wide[0:BLOCK] + wide[BLOCK : 2 * BLOCK] + wide[2 * BLOCK :]
            ref[b, :, 0 : 4 * BLOCK] = wide[:, : 4 * BLOCK]
            ref[b, :, 4 * BLOCK : 5 * BLOCK] = mine
            ref[b, :, 5 * BLOCK :] = wide[:, 4 * BLOCK :]


def solve_kernel(nx, ny, f_ref, m_ref, n_ref, k_ref, mean_ref, res_ref, *scratch):
    (res, terms, terms_in, total, image, image_in, sums, sums_y, sums_x) = scratch[:9]
    (send_t, recv_t, send_i, recv_i, send_y, recv_y, send_x, recv_x) = scratch[9:]
    links = Links(nx, ny)
    gx, gy = links.x, links.y
    barrier = pltpu.get_barrier_semaphore()
    corners = links.greet(barrier, [k for k in range(8) if 0 not in DIRS[k]])
    line_y = [(gx, lax.rem(gy + off, ny)) for off in range(1, ny)]
    line_x = [(lax.rem(gx + off, nx), gy) for off in range(1, nx)]
    for peer in line_y + line_x:
        pl.semaphore_signal(barrier, inc=1, device_id=peer, device_id_type=MESH)
    for cell in range(16):
        res[cell : cell + 1, :] = f_ref[4:5, cell * BLOCK : (cell + 1) * BLOCK]
    noise = [f_ref[3:4, c * BLOCK : (c + 1) * BLOCK] for c in OWN]

    def precondition(step):
        out = [jnp.zeros((1, BLOCK), jnp.float32) for _ in range(16)]
        for b in range(4):
            acc = jnp.zeros((BLOCK, BLOCK), jnp.float32)
            for q, cell in enumerate(around(b)):
                acc = acc + m_ref[b, :, q * BLOCK : (q + 1) * BLOCK] * res[cell : cell + 1, :]
            w = jnp.sum(acc, axis=1, keepdims=True)
            for q, cell in enumerate(around(b)):
                part = n_ref[b, :, q * BLOCK : (q + 1) * BLOCK] * w
                out[cell] = out[cell] + jnp.sum(part, axis=0, keepdims=True)
        for cell in range(16):
            terms[step, cell : cell + 1, :] = out[cell]

    def exchange_terms(step):
        args = (terms.at[step], terms_in.at[step], send_t.at[step], recv_t.at[step])
        links.start(*args)
        links.finish(*args)
        for cell in range(16):
            r, c = cell // 4, cell % 4
            value = terms[step, cell : cell + 1, :]
            for k, (dx, dy) in enumerate(DIRS):
                rr, cc = r - 2 * dx, c - 2 * dy
                if 0 <= rr < 4 and 0 <= cc < 4:
                    at = rr * 4 + cc
                    value = value + terms_in[step, k, at : at + 1, :]
            total[step, cell : cell + 1, :] = value

    def operate(step):
        columns = total[step].T
        for b in range(4):
            acc = jnp.zeros((BLOCK, BLOCK), jnp.float32)
            for q, cell in enumerate(around(b)):
                acc = acc + k_ref[b, q * BLOCK : (q + 1) * BLOCK, :] * columns[:, cell : cell + 1]
            value = jnp.sum(acc, axis=0, keepdims=True)
            value = value + noise[b] * total[step, OWN[b] : OWN[b] + 1, :]
            image[step, b : b + 1, :] = value

    def line_copy(step, buf, send, recv, peer, at, off):
        return pltpu.make_async_remote_copy(
            src_ref=sums.at[step, 0] if buf is sums_y else sums.at[step, 1],
            dst_ref=buf.at[step, at],
            send_sem=send.at[step, off],
            recv_sem=recv.at[step, off],
            device_id=peer,
            device_id_type=MESH,
        )

    def reduce_line(step, buf, send, recv, peers, me, size):
        copies = [line_copy(step, buf, send, recv, p, me, o) for o, p in enumerate(peers)]
        for copy in copies:
            copy.start()
        buf[step, me] = sums[step, 0] if buf is sums_y else sums[step, 1]
        for copy in copies:
            copy.wait()
        value = buf[step, 0]
        for at in range(1, size):
            value = value + buf[step, at]
        return value

    def reduce_all(step, *rows):
        sums[step, 0] = jnp.zeros((8, BLOCK), jnp.float32)
        for at, row in enumerate(rows):
            sums[step, 0, at : at + 1, :] = row
        sums[step, 1] = reduce_line(step, sums_y, send_y, recv_y, line_y, gy, ny)
        value = reduce_line(step, sums_x, send_x, recv_x, line_x, gx, nx)
        value = jnp.sum(value, axis=1, keepdims=True)
        return [value[at : at + 1, :] for at in range(len(rows))]

    def across(pairs):
        value = pairs[0][0] * pairs[0][1]
        for a, b in pairs[1:]:
            value = value + a * b
        return value

    def mine(ref, step):
        return [ref[step, c : c + 1, :] for c in OWN]

    precondition(0)
    pl.semaphore_wait(barrier, corners + nx + ny - 2)
    exchange_terms(0)
    image[...] = jnp.zeros_like(image)
    operate(0)
    args = (image.at[0], image_in, send_i, recv_i)
    links.start(*args)
    first = mine(total, 0)
    along = [image[0, b : b + 1, :] for b in range(4)]
    start = [res[c : c + 1, :] for c in OWN]
    current, curve = reduce_all(
        0, across(list(zip(start, first))), across(list(zip(first, along)))
    )
    links.finish(*args)
    alpha = current / curve
    for cell in range(16):
        way, inner = source_of(cell)
        if way == (0, 0):
            value = image[0, inner : inner + 1, :]
        else:
            value = image_in[DIRS.index(way), inner : inner + 1, :]
        res[cell : cell + 1, :] = res[cell : cell + 1, :] - alpha * value
    precondition(1)
    exchange_terms(1)
    operate(1)
    second = mine(total, 1)
    along2 = [image[1, b : b + 1, :] for b in range(4)]
    left = [res[c : c + 1, :] for c in OWN]
    following, own_curve, cross = reduce_all(
        1,
        across(list(zip(left, second))),
        across(list(zip(second, along2))),
        across(list(zip(second, along))),
    )
    ratio = following / current
    alpha2 = following / (own_curve + ratio * (2.0 * cross + ratio * curve))
    for b in range(4):
        solved = alpha * first[b] + alpha2 * (second[b] + ratio * first[b])
        mean_ref[b : b + 1, :] = start[b] - noise[b] * solved
        res_ref[b : b + 1, :] = left[b] - alpha2 * (along2[b] + ratio * along[b])


def local(nx, ny, coords, neighbours, noise_var, observations):
    tile = observations.shape[2]
    f32 = jnp.float32
    vmem = pl.BlockSpec(memory_space=pltpu.VMEM)
    dma = pltpu.SemaphoreType.DMA
    listed = neighbours.reshape(4, NEIGH)
    slot, within = listed // tile, listed % tile
    row = (slot // 3) * 2 + within // (2 * BLOCK) - 1
    col = (slot % 3) * 2 + (within // BLOCK) % 2 - 1
    index = jnp.where(listed >= 0, (row * 4 + col) * BLOCK + within % BLOCK, -1)
    index = jnp.pad(index, ((0, 4), (0, 0)))
    patch = pl.pallas_call(
        functools.partial(halo_kernel, nx, ny),
        out_shape=jax.ShapeDtypeStruct((8, 16 * BLOCK), f32),
        in_specs=[vmem] * 3,
        out_specs=vmem,
        scratch_shapes=[
            pltpu.VMEM((8, tile), f32),
            pltpu.VMEM((8, 8, tile), f32),
            dma((8,)),
            dma((8,)),
        ],
        compiler_params=pltpu.CompilerParams(collective_id=0, has_side_effects=True),
        name="halo",
    )(coords.reshape(3, tile), noise_var.reshape(1, tile), observations.reshape(1, tile))
    wide = jax.ShapeDtypeStruct((4, BLOCK, 9 * BLOCK), f32)
    square = pltpu.VMEM((4, BLOCK, BLOCK), f32)
    m, n, k = pl.pallas_call(
        factor_kernel,
        out_shape=(wide, wide, jax.ShapeDtypeStruct((4, 9 * BLOCK, BLOCK), f32)),
        in_specs=[vmem] * 2,
        out_specs=[vmem] * 3,
        scratch_shapes=[
            square,
            pltpu.VMEM((4, NEIGH, 8 * BLOCK), jnp.bfloat16),
            pltpu.VMEM((4, NEIGH, NEIGH), f32),
            pltpu.VMEM((4, BLOCK, NEIGH), f32),
            square,
            square,
            square,
            pltpu.VMEM((256, BLOCK), f32),
        ],
        compiler_params=pltpu.CompilerParams(vmem_limit_bytes=48 << 20),
        name="factor",
    )(patch, index)
    mean, residual = pl.pallas_call(
        functools.partial(solve_kernel, nx, ny),
        out_shape=(jax.ShapeDtypeStruct((4, BLOCK), f32),) * 2,
        in_specs=[vmem] * 4,
        out_specs=[vmem] * 2,
        scratch_shapes=[
            pltpu.VMEM((16, BLOCK), f32),
            pltpu.VMEM((2, 16, BLOCK), f32),
            pltpu.VMEM((2, 8, 16, BLOCK), f32),
            pltpu.VMEM((2, 16, BLOCK), f32),
            pltpu.VMEM((2, 8, BLOCK), f32),
            pltpu.VMEM((8, 8, BLOCK), f32),
            pltpu.VMEM((2, 2, 8, BLOCK), f32),
            pltpu.VMEM((2, ny, 8, BLOCK), f32),
            pltpu.VMEM((2, nx, 8, BLOCK), f32),
            dma((2, 8)),
            dma((2, 8)),
            dma((8,)),
            dma((8,)),
            dma((2, ny)),
            dma((2, ny)),
            dma((2, nx)),
            dma((2, nx)),
        ],
        compiler_params=pltpu.CompilerParams(
            collective_id=1, has_side_effects=True, vmem_limit_bytes=48 << 20
        ),
        name="solve",
    )(patch, m, n, k)
    return (mean.reshape(observations.shape), residual.reshape(observations.shape))


def solution(mesh):
    in_specs = (
        P(None, "gx", "gy", None),
        P("gx", "gy", None, None),
        P("gx", "gy", None),
        P("gx", "gy", None),
    )
    out_specs = (P("gx", "gy", None), P("gx", "gy", None))
    body = functools.partial(local, mesh.shape["gx"], mesh.shape["gy"])
    return jax.shard_map(body, mesh=mesh, in_specs=in_specs, out_specs=out_specs, check_vma=False)
```

```python
import functools

import jax
import jax.numpy as jnp
from jax import lax
from jax.experimental import pallas as pl
from jax.experimental.pallas import tpu as pltpu
from jax.sharding import PartitionSpec as P

MESH = pl.DeviceIdType.MESH
BLOCK = 128
NEIGH = 256
HIGH = lax.Precision.HIGHEST
DIRS = [(dx, dy) for dx in (-1, 0, 1) for dy in (-1, 0, 1) if (dx, dy) != (0, 0)]
OWN = [5, 6, 9, 10]


def around(b):
    r, c = 1 + b // 2, 1 + b % 2
    return [(r - 1 + q // 3) * 4 + c - 1 + q % 3 for q in range(9)]


def others(b):
    return [cell for q, cell in enumerate(around(b)) if q != 4]


class Links:
    def __init__(self, nx, ny):
        self.nx, self.ny = nx, ny
        self.x, self.y = lax.axis_index("gx"), lax.axis_index("gy")

    def there(self, k):
        dx, dy = DIRS[k]
        px, py = self.x + dx, self.y + dy
        return (px >= 0) & (px < self.nx) & (py >= 0) & (py < self.ny)

    def ident(self, k):
        return (self.x + DIRS[k][0], self.y + DIRS[k][1])

    def copy(self, k, slot, src, dst, send, recv):
        return pltpu.make_async_remote_copy(
            src_ref=src,
            dst_ref=dst.at[slot],
            send_sem=send.at[k],
            recv_sem=recv.at[slot],
            device_id=self.ident(k),
            device_id_type=MESH,
        )

    def start(self, src, dst, send, recv):
        for k in range(8):

            @pl.when(self.there(k))
            def _():
                self.copy(k, 7 - k, src, dst, send, recv).start()

            @pl.when(jnp.logical_not(self.there(k)))
            def _():
                dst[k] = jnp.zeros(dst.shape[1:], dst.dtype)

    def finish(self, src, dst, send, recv):
        for k in range(8):

            @pl.when(self.there(k))
            def _():
                desc = self.copy(k, k, src, dst, send, recv)
                desc.wait_send()
                desc.wait_recv()

    def greet(self, barrier, ways=range(8)):
        count = 0
        for k in ways:
            count = count + self.there(k).astype(jnp.int32)

            @pl.when(self.there(k))
            def _():
                pl.semaphore_signal(
                    barrier, inc=1, device_id=self.ident(k), device_id_type=MESH
                )

        return count


def source_of(cell):
    row, col = cell // 4 + 1, cell % 4 + 1
    dx, dy = row // 2 - 1, col // 2 - 1
    return (dx, dy), (row % 2) * 2 + col % 2


def halo_kernel(nx, ny, coords, noise, obs, out, own, land, send, recv):
    links = Links(nx, ny)
    own[...] = jnp.zeros_like(own)
    for axis in range(3):
        own[axis : axis + 1, :] = coords[axis, 0]
    own[3:4, :] = noise[...]
    own[4:5, :] = obs[...]
    barrier = pltpu.get_barrier_semaphore()
    pl.semaphore_wait(barrier, links.greet(barrier))
    links.start(own, land, send, recv)
    links.finish(own, land, send, recv)
    for cell in range(16):
        way, inner = source_of(cell)
        part = slice(inner * BLOCK, (inner + 1) * BLOCK)
        value = own[:, part] if way == (0, 0) else land[DIRS.index(way), :, part]
        out[:, cell * BLOCK : (cell + 1) * BLOCK] = value


def kernel_value(ax, ay, at, bx, by, bt):
    dx, dy = ax - bx, ay - by
    distance = jnp.sqrt(dx * dx + dy * dy)
    inside = jnp.maximum(1.0 - distance, 0.0)
    square = inside * inside
    return square * square * (4.0 * distance + 1.0) * jnp.exp(-jnp.abs(at - bt))


def thirds(x):
    high = x.astype(jnp.bfloat16).astype(jnp.float32)
    rest = x - high
    mid = rest.astype(jnp.bfloat16).astype(jnp.float32)
    return high, mid, rest - mid


def dot(a, b, rhs=0):
    return lax.dot_general(
        a, b, (((1,), (rhs,)), ((), ())), precision=HIGH, preferred_element_type=jnp.float32
    )


def pick(a, b, rhs=0):
    return lax.dot_general(
        a, b, (((1,), (rhs,)), ((), ())), preferred_element_type=jnp.float32
    )


def iota(shape, axis):
    return lax.broadcasted_iota(jnp.int32, shape, axis)


def invert(a_ref, count, mix):
    f32 = jnp.float32
    lanes = iota((1, BLOCK), 1)
    keep = lanes >= 8

    def shift(x):
        return pltpu.roll(x, BLOCK - 8, axis=1)

    def panel(p, base):
        d = [
            [jnp.broadcast_to(p[i][:, base + j : base + j + 1], (8, BLOCK)) for j in range(i + 1)]
            for i in range(8)
        ]
        if base:
            p = [shift(x) for x in p]
        y = [jnp.where(keep, p[i], (lanes == i).astype(f32)) for i in range(8)]
        low = [[None] * 8 for _ in range(8)]
        inverse = [None] * 8
        for j in range(8):
            inverse[j] = 1.0 / d[j][j]
            for i in range(j + 1, 8):
                low[i][j] = d[i][j] * inverse[j]
            for i in range(j + 1, 8):
                for k in range(j + 1, i + 1):
                    d[i][k] = d[i][k] - low[i][j] * d[k][j]
            for i in range(j + 1, 8):
                y[i] = y[i] - low[i][j] * y[j]
        u = [y[j] * inverse[j] for j in range(8)]
        for j in range(7, 0, -1):
            for i in range(j):
                u[i] = u[i] - low[j][i] * u[j]
        return u

    def advance(rows, u):
        out = []
        for row in rows:
            t = [row[:, k : k + 1] * u[k] for k in range(8)]
            total = ((t[0] + t[1]) + (t[2] + t[3])) + ((t[4] + t[5]) + (t[6] + t[7]))
            out.append(jnp.where(keep, row, 0.0) - total)
        return out

    def pack(place, b, tile):
        mix[pl.ds(place * 64 + b, 8, stride=8), :] = tile

    def unpack(place, b):
        return mix[pl.ds(place * 64 + b, 8, stride=8), :]

    def load(place):
        return [mix[place * 64 + i * 8 : place * 64 + (i + 1) * 8, :] for i in range(8)]

    def save(place, u):
        for i in range(8):
            mix[place * 64 + i * 8 : place * 64 + (i + 1) * 8, :] = u[i]

    def rest(first):
        for b in range(count):
            u = shift(unpack(3, b))
            old = a_ref[b, first * 8 :, :]
            new = shift(jnp.where(keep, old, 0.0)) - dot(old[:, 0:8], u)
            a_ref[b, first * 8 - 8 : BLOCK - 8, :] = new
            a_ref[b, BLOCK - 8 :, :] = u
            pack(2, b, new[0:8])

    for place in range(3):
        for b in range(8):
            pack(place, b, a_ref[b % count, place * 8 : place * 8 + 8, :])
    u = panel(load(0), 0)
    n = advance(load(1), u)
    save(3, u)

    def turn(_, carry):
        n, before = carry[:8], carry[8:]
        q = [shift(x) for x in advance(load(2), before)]
        u = panel(n, 8)
        rest(3)
        n = advance(q, u)
        save(3, u)
        return tuple(n) + tuple(u)

    carry = lax.fori_loop(0, BLOCK // 8 - 1, turn, tuple(n) + tuple(u))
    rest(2)
    save(0, [shift(x) for x in carry[:8]])
    for b in range(count):
        a_ref[b, 0:8, :] = unpack(0, b)


def factor_kernel(f_ref, listed_ref, m_ref, n_ref, a_ref, hot, c11, c21, c22, w2, w3, *room):
    count = 4
    listed = listed_ref[0, 0]
    slot, within = listed >> 9, listed & 511
    third = (slot * 11) >> 5
    row = third * 2 + (within >> 8) - 1
    col = (slot - 3 * third) * 2 + ((within >> 7) & 1) - 1
    index = jnp.where(listed >= 0, (row * 4 + col) * BLOCK + (within & 127), -1)
    idx = index.astype(jnp.float32)
    idx = jnp.concatenate([idx, idx], axis=0)
    idx_t = idx.T
    lane = iota((1, BLOCK), 1).astype(jnp.float32)
    for b in range(count):
        chosen = idx_t[:, b : b + 1]
        for q, cell in enumerate(others(b)):
            same = chosen == lane + float(cell * BLOCK)
            hot[b, :, q * BLOCK : (q + 1) * BLOCK] = same.astype(jnp.float32).astype(jnp.bfloat16)
        near = jnp.concatenate(
            [f_ref[:, cell * BLOCK : (cell + 1) * BLOCK] for cell in others(b)], axis=1
        )
        stacked = jnp.concatenate([*thirds(near), jnp.zeros_like(near)], axis=0)
        found = pick(stacked.astype(jnp.bfloat16), hot[b], 1)
        x = found[0:8] + found[8:16] + found[16:24]
        xt = x.T
        live_row = (idx[b : b + 1, :] >= 0.0).astype(jnp.float32)
        live_col = (chosen >= 0.0).astype(jnp.float32)
        diagonal = live_row * x[3:4] + (1.0 - live_row)
        on_diagonal = iota((NEIGH, NEIGH), 0) == iota((NEIGH, NEIGH), 1)
        kern = kernel_value(xt[:, 0:1], xt[:, 1:2], xt[:, 2:3], x[0:1], x[1:2], x[2:3])
        c11[b] = kern * live_col * live_row + jnp.where(on_diagonal, diagonal, 0.0)
        home = OWN[b] * BLOCK
        o = f_ref[:, home : home + BLOCK]
        ot = o.T
        kern = kernel_value(ot[:, 0:1], ot[:, 1:2], ot[:, 2:3], x[0:1], x[1:2], x[2:3])
        c21[b] = kern * live_row
        on_diagonal = iota((BLOCK, BLOCK), 0) == iota((BLOCK, BLOCK), 1)
        kern = kernel_value(ot[:, 0:1], ot[:, 1:2], ot[:, 2:3], o[0:1], o[1:2], o[2:3])
        c22[b] = kern + jnp.where(on_diagonal, o[3:4], 0.0)
        a_ref[b] = c11[b, 0:BLOCK, 0:BLOCK]
    invert(a_ref, count, *room)
    for b in range(count):
        inverse = a_ref[b]
        a21 = c11[b, BLOCK:, 0:BLOCK]
        own1 = c21[b, :, 0:BLOCK]
        left2, left3 = dot(a21, inverse), dot(own1, inverse)
        w2[b], w3[b] = left2, left3
        a_ref[b] = c11[b, BLOCK:, BLOCK:] - dot(left2, a21, 1)
        c21[b, :, BLOCK:] = c21[b, :, BLOCK:] - dot(left3, a21, 1)
        c22[b] = c22[b] - dot(left3, own1, 1)
    invert(a_ref, count, *room)
    for b in range(count):
        own2 = c21[b, :, BLOCK:]
        b2 = dot(own2, a_ref[b])
        c21[b, :, 0:BLOCK] = dot(b2, w2[b]) - w3[b]
        a_ref[b] = c22[b] - dot(b2, own2, 1)
        c21[b, :, BLOCK:] = -b2
    invert(a_ref, count, *room)
    eye = (iota((BLOCK, BLOCK), 0) == iota((BLOCK, BLOCK), 1)).astype(jnp.float32)
    for b in range(count):
        inverse = a_ref[b]
        compact = c21[b]
        for ref, mine, theirs in ((m_ref, eye, compact), (n_ref, inverse, dot(inverse, compact))):
            stacked = jnp.concatenate(thirds(theirs), axis=0).astype(jnp.bfloat16)
            wide = pick(stacked, hot[b])
            wide = wide[0:BLOCK] + wide[BLOCK : 2 * BLOCK] + wide[2 * BLOCK :]
            ref[b, :, 0 : 4 * BLOCK] = wide[:, : 4 * BLOCK]
            ref[b, :, 4 * BLOCK : 5 * BLOCK] = mine
            ref[b, :, 5 * BLOCK :] = wide[:, 4 * BLOCK :]


def solve_kernel(nx, ny, f_ref, m_ref, n_ref, mean_ref, res_ref, k_ref, *scratch):
    (res, terms, terms_in, total, image, image_in, sums, sums_y, sums_x) = scratch[:9]
    (send_t, recv_t, send_i, recv_i, send_y, recv_y, send_x, recv_x) = scratch[9:]
    links = Links(nx, ny)
    gx, gy = links.x, links.y
    barrier = pltpu.get_barrier_semaphore()
    corners = links.greet(barrier, [k for k in range(8) if 0 not in DIRS[k]])
    line_y = [(gx, lax.rem(gy + off, ny)) for off in range(1, ny)]
    line_x = [(lax.rem(gx + off, nx), gy) for off in range(1, nx)]
    for peer in line_y + line_x:
        pl.semaphore_signal(barrier, inc=1, device_id=peer, device_id_type=MESH)
    for cell in range(16):
        res[cell : cell + 1, :] = f_ref[4:5, cell * BLOCK : (cell + 1) * BLOCK]
    noise = [f_ref[3:4, c * BLOCK : (c + 1) * BLOCK] for c in OWN]

    def precondition(step):
        out = [jnp.zeros((1, BLOCK), jnp.float32) for _ in range(16)]
        for b in range(4):
            acc = jnp.zeros((BLOCK, BLOCK), jnp.float32)
            for q, cell in enumerate(around(b)):
                acc = acc + m_ref[b, :, q * BLOCK : (q + 1) * BLOCK] * res[cell : cell + 1, :]
            w = jnp.sum(acc, axis=1, keepdims=True)
            for q, cell in enumerate(around(b)):
                part = n_ref[b, :, q * BLOCK : (q + 1) * BLOCK] * w
                out[cell] = out[cell] + jnp.sum(part, axis=0, keepdims=True)
        for cell in range(16):
            terms[step, cell : cell + 1, :] = out[cell]

    def fill_kernel():
        parts = [f_ref[:, cell * BLOCK : (cell + 1) * BLOCK] for cell in range(16)]
        turned = [part.T for part in parts]
        for b in range(4):
            o = parts[OWN[b]]
            for q, cell in enumerate(around(b)):
                t = turned[cell]
                kern = kernel_value(t[:, 0:1], t[:, 1:2], t[:, 2:3], o[0:1], o[1:2], o[2:3])
                k_ref[b, q * BLOCK : (q + 1) * BLOCK, :] = kern

    def exchange_terms(step):
        args = (terms.at[step], terms_in.at[step], send_t.at[step], recv_t.at[step])
        links.start(*args)
        if step == 0:
            fill_kernel()
        links.finish(*args)
        for cell in range(16):
            r, c = cell // 4, cell % 4
            value = terms[step, cell : cell + 1, :]
            for k, (dx, dy) in enumerate(DIRS):
                rr, cc = r - 2 * dx, c - 2 * dy
                if 0 <= rr < 4 and 0 <= cc < 4:
                    at = rr * 4 + cc
                    value = value + terms_in[step, k, at : at + 1, :]
            total[step, cell : cell + 1, :] = value

    def operate(step):
        columns = total[step].T
        for b in range(4):
            acc = jnp.zeros((BLOCK, BLOCK), jnp.float32)
            for q, cell in enumerate(around(b)):
                acc = acc + k_ref[b, q * BLOCK : (q + 1) * BLOCK, :] * columns[:, cell : cell + 1]
            value = jnp.sum(acc, axis=0, keepdims=True)
            value = value + noise[b] * total[step, OWN[b] : OWN[b] + 1, :]
            image[step, b : b + 1, :] = value

    def line_copy(step, buf, send, recv, peer, at, off):
        return pltpu.make_async_remote_copy(
            src_ref=sums.at[step, 0] if buf is sums_y else sums.at[step, 1],
            dst_ref=buf.at[step, at],
            send_sem=send.at[step, off],
            recv_sem=recv.at[step, off],
            device_id=peer,
            device_id_type=MESH,
        )

    def reduce_line(step, buf, send, recv, peers, me, size):
        copies = [line_copy(step, buf, send, recv, p, me, o) for o, p in enumerate(peers)]
        for copy in copies:
            copy.start()
        buf[step, me] = sums[step, 0] if buf is sums_y else sums[step, 1]
        for copy in copies:
            copy.wait()
        value = buf[step, 0]
        for at in range(1, size):
            value = value + buf[step, at]
        return value

    def reduce_all(step, *rows):
        sums[step, 0] = jnp.zeros((8, BLOCK), jnp.float32)
        for at, row in enumerate(rows):
            sums[step, 0, at : at + 1, :] = row
        sums[step, 1] = reduce_line(step, sums_y, send_y, recv_y, line_y, gy, ny)
        value = reduce_line(step, sums_x, send_x, recv_x, line_x, gx, nx)
        value = jnp.sum(value, axis=1, keepdims=True)
        return [value[at : at + 1, :] for at in range(len(rows))]

    def across(pairs):
        value = pairs[0][0] * pairs[0][1]
        for a, b in pairs[1:]:
            value = value + a * b
        return value

    def mine(ref, step):
        return [ref[step, c : c + 1, :] for c in OWN]

    precondition(0)
    pl.semaphore_wait(barrier, corners + nx + ny - 2)
    exchange_terms(0)
    image[...] = jnp.zeros_like(image)
    operate(0)
    args = (image.at[0], image_in, send_i, recv_i)
    links.start(*args)
    first = mine(total, 0)
    along = [image[0, b : b + 1, :] for b in range(4)]
    start = [res[c : c + 1, :] for c in OWN]
    current, curve = reduce_all(
        0, across(list(zip(start, first))), across(list(zip(first, along)))
    )
    links.finish(*args)
    alpha = current / curve
    for cell in range(16):
        way, inner = source_of(cell)
        if way == (0, 0):
            value = image[0, inner : inner + 1, :]
        else:
            value = image_in[DIRS.index(way), inner : inner + 1, :]
        res[cell : cell + 1, :] = res[cell : cell + 1, :] - alpha * value
    precondition(1)
    exchange_terms(1)
    operate(1)
    second = mine(total, 1)
    along2 = [image[1, b : b + 1, :] for b in range(4)]
    left = [res[c : c + 1, :] for c in OWN]
    following, own_curve, cross = reduce_all(
        1,
        across(list(zip(left, second))),
        across(list(zip(second, along2))),
        across(list(zip(second, along))),
    )
    ratio = following / current
    alpha2 = following / (own_curve + ratio * (2.0 * cross + ratio * curve))
    for b in range(4):
        solved = alpha * first[b] + alpha2 * (second[b] + ratio * first[b])
        mean_ref[b : b + 1, :] = start[b] - noise[b] * solved
        res_ref[b : b + 1, :] = left[b] - alpha2 * (along2[b] + ratio * along[b])


def local(nx, ny, coords, neighbours, noise_var, observations):
    tile = observations.shape[2]
    f32 = jnp.float32
    vmem = pl.BlockSpec(memory_space=pltpu.VMEM)
    dma = pltpu.SemaphoreType.DMA
    patch = pl.pallas_call(
        functools.partial(halo_kernel, nx, ny),
        out_shape=jax.ShapeDtypeStruct((8, 16 * BLOCK), f32),
        in_specs=[vmem] * 3,
        out_specs=vmem,
        scratch_shapes=[
            pltpu.VMEM((8, tile), f32),
            pltpu.VMEM((8, 8, tile), f32),
            dma((8,)),
            dma((8,)),
        ],
        compiler_params=pltpu.CompilerParams(collective_id=0, has_side_effects=True),
        name="halo",
    )(coords, noise_var.reshape(1, tile), observations.reshape(1, tile))
    wide = jax.ShapeDtypeStruct((4, BLOCK, 9 * BLOCK), f32)
    square = pltpu.VMEM((4, BLOCK, BLOCK), f32)
    m, n = pl.pallas_call(
        factor_kernel,
        out_shape=(wide, wide),
        in_specs=[vmem] * 2,
        out_specs=[vmem] * 2,
        scratch_shapes=[
            square,
            pltpu.VMEM((4, NEIGH, 8 * BLOCK), jnp.bfloat16),
            pltpu.VMEM((4, NEIGH, NEIGH), f32),
            pltpu.VMEM((4, BLOCK, NEIGH), f32),
            square,
            square,
            square,
            pltpu.VMEM((256, BLOCK), f32),
        ],
        compiler_params=pltpu.CompilerParams(vmem_limit_bytes=48 << 20),
        name="factor",
    )(patch, neighbours)
    mean, residual = pl.pallas_call(
        functools.partial(solve_kernel, nx, ny),
        out_shape=(jax.ShapeDtypeStruct((4, BLOCK), f32),) * 2,
        in_specs=[vmem] * 3,
        out_specs=[vmem] * 2,
        scratch_shapes=[
            pltpu.VMEM((4, 9 * BLOCK, BLOCK), f32),
            pltpu.VMEM((16, BLOCK), f32),
            pltpu.VMEM((2, 16, BLOCK), f32),
            pltpu.VMEM((2, 8, 16, BLOCK), f32),
            pltpu.VMEM((2, 16, BLOCK), f32),
            pltpu.VMEM((2, 8, BLOCK), f32),
            pltpu.VMEM((8, 8, BLOCK), f32),
            pltpu.VMEM((2, 2, 8, BLOCK), f32),
            pltpu.VMEM((2, ny, 8, BLOCK), f32),
            pltpu.VMEM((2, nx, 8, BLOCK), f32),
            dma((2, 8)),
            dma((2, 8)),
            dma((8,)),
            dma((8,)),
            dma((2, ny)),
            dma((2, ny)),
            dma((2, nx)),
            dma((2, nx)),
        ],
        compiler_params=pltpu.CompilerParams(
            collective_id=1, has_side_effects=True, vmem_limit_bytes=48 << 20
        ),
        name="solve",
    )(patch, m, n)
    return (mean.reshape(observations.shape), residual.reshape(observations.shape))


def solution(mesh):
    in_specs = (
        P(None, "gx", "gy", None),
        P("gx", "gy", None, None),
        P("gx", "gy", None),
        P("gx", "gy", None),
    )
    out_specs = (P("gx", "gy", None), P("gx", "gy", None))
    body = functools.partial(local, mesh.shape["gx"], mesh.shape["gy"])
    return jax.shard_map(body, mesh=mesh, in_specs=in_specs, out_specs=out_specs, check_vma=False)
```

```python
import functools

import jax
import jax.numpy as jnp
from jax import lax
from jax.experimental import pallas as pl
from jax.experimental.pallas import tpu as pltpu
from jax.sharding import PartitionSpec as P

MESH = pl.DeviceIdType.MESH
BLOCK = 128
NEIGH = 256
HIGH = lax.Precision.HIGHEST
DIRS = [(dx, dy) for dx in (-1, 0, 1) for dy in (-1, 0, 1) if (dx, dy) != (0, 0)]
OWN = [5, 6, 9, 10]


def around(b):
    r, c = 1 + b // 2, 1 + b % 2
    return [(r - 1 + q // 3) * 4 + c - 1 + q % 3 for q in range(9)]


def others(b):
    return [cell for q, cell in enumerate(around(b)) if q != 4]


class Links:
    def __init__(self, nx, ny):
        self.nx, self.ny = nx, ny
        self.x, self.y = lax.axis_index("gx"), lax.axis_index("gy")

    def there(self, k):
        dx, dy = DIRS[k]
        px, py = self.x + dx, self.y + dy
        return (px >= 0) & (px < self.nx) & (py >= 0) & (py < self.ny)

    def ident(self, k):
        return (self.x + DIRS[k][0], self.y + DIRS[k][1])

    def copy(self, k, slot, src, dst, send, recv):
        return pltpu.make_async_remote_copy(
            src_ref=src,
            dst_ref=dst.at[slot],
            send_sem=send.at[k],
            recv_sem=recv.at[slot],
            device_id=self.ident(k),
            device_id_type=MESH,
        )

    def start(self, src, dst, send, recv):
        for k in range(8):

            @pl.when(self.there(k))
            def _():
                self.copy(k, 7 - k, src, dst, send, recv).start()

            @pl.when(jnp.logical_not(self.there(k)))
            def _():
                dst[k] = jnp.zeros(dst.shape[1:], dst.dtype)

    def finish(self, src, dst, send, recv):
        for k in range(8):

            @pl.when(self.there(k))
            def _():
                desc = self.copy(k, k, src, dst, send, recv)
                desc.wait_send()
                desc.wait_recv()

    def greet(self, barrier, ways=range(8)):
        count = 0
        for k in ways:
            count = count + self.there(k).astype(jnp.int32)

            @pl.when(self.there(k))
            def _():
                pl.semaphore_signal(
                    barrier, inc=1, device_id=self.ident(k), device_id_type=MESH
                )

        return count


def source_of(cell):
    row, col = cell // 4 + 1, cell % 4 + 1
    dx, dy = row // 2 - 1, col // 2 - 1
    return (dx, dy), (row % 2) * 2 + col % 2


def halo_kernel(nx, ny, coords, noise, obs, out, own, land, send, recv):
    links = Links(nx, ny)
    barrier = pltpu.get_barrier_semaphore()
    greeted = links.greet(barrier)
    own[...] = jnp.zeros_like(own)
    for axis in range(3):
        own[axis : axis + 1, :] = coords[axis, 0]
    own[3:4, :] = noise[...]
    own[4:5, :] = obs[...]
    pl.semaphore_wait(barrier, greeted)
    links.start(own, land, send, recv)
    links.finish(own, land, send, recv)
    for cell in range(16):
        way, inner = source_of(cell)
        part = slice(inner * BLOCK, (inner + 1) * BLOCK)
        value = own[:, part] if way == (0, 0) else land[DIRS.index(way), :, part]
        out[:, cell * BLOCK : (cell + 1) * BLOCK] = value


def kernel_value(ax, ay, at, bx, by, bt):
    dx, dy = ax - bx, ay - by
    distance = jnp.sqrt(dx * dx + dy * dy)
    inside = jnp.maximum(1.0 - distance, 0.0)
    square = inside * inside
    return square * square * (4.0 * distance + 1.0) * jnp.exp(-jnp.abs(at - bt))


def thirds(x):
    high = x.astype(jnp.bfloat16).astype(jnp.float32)
    rest = x - high
    mid = rest.astype(jnp.bfloat16).astype(jnp.float32)
    return high, mid, rest - mid


def dot(a, b, rhs=0):
    return lax.dot_general(
        a, b, (((1,), (rhs,)), ((), ())), precision=HIGH, preferred_element_type=jnp.float32
    )


def pick(a, b, rhs=0):
    return lax.dot_general(
        a, b, (((1,), (rhs,)), ((), ())), preferred_element_type=jnp.float32
    )


def iota(shape, axis):
    return lax.broadcasted_iota(jnp.int32, shape, axis)


def invert(a_ref, count, mix):
    f32 = jnp.float32
    lanes = iota((1, BLOCK), 1)
    keep = lanes >= 8

    def shift(x):
        return pltpu.roll(x, BLOCK - 8, axis=1)

    def panel(p, base):
        d = [
            [jnp.broadcast_to(p[i][:, base + j : base + j + 1], (8, BLOCK)) for j in range(i + 1)]
            for i in range(8)
        ]
        if base:
            p = [shift(x) for x in p]
        y = [jnp.where(keep, p[i], (lanes == i).astype(f32)) for i in range(8)]
        low = [[None] * 8 for _ in range(8)]
        inverse = [None] * 8
        for j in range(8):
            inverse[j] = 1.0 / d[j][j]
            for i in range(j + 1, 8):
                low[i][j] = d[i][j] * inverse[j]
            for i in range(j + 1, 8):
                for k in range(j + 1, i + 1):
                    d[i][k] = d[i][k] - low[i][j] * d[k][j]
            for i in range(j + 1, 8):
                y[i] = y[i] - low[i][j] * y[j]
        u = [y[j] * inverse[j] for j in range(8)]
        for j in range(7, 0, -1):
            for i in range(j):
                u[i] = u[i] - low[j][i] * u[j]
        return u

    def advance(rows, u):
        out = []
        for row in rows:
            t = [row[:, k : k + 1] * u[k] for k in range(8)]
            total = ((t[0] + t[1]) + (t[2] + t[3])) + ((t[4] + t[5]) + (t[6] + t[7]))
            out.append(jnp.where(keep, row, 0.0) - total)
        return out

    def pack(place, b, tile):
        mix[pl.ds(place * 64 + b, 8, stride=8), :] = tile

    def unpack(place, b):
        return mix[pl.ds(place * 64 + b, 8, stride=8), :]

    def load(place):
        return [mix[place * 64 + i * 8 : place * 64 + (i + 1) * 8, :] for i in range(8)]

    def save(place, u):
        for i in range(8):
            mix[place * 64 + i * 8 : place * 64 + (i + 1) * 8, :] = u[i]

    def rest(first):
        for b in range(count):
            u = shift(unpack(3, b))
            old = a_ref[b, first * 8 :, :]
            new = shift(jnp.where(keep, old, 0.0)) - dot(old[:, 0:8], u)
            a_ref[b, first * 8 - 8 : BLOCK - 8, :] = new
            a_ref[b, BLOCK - 8 :, :] = u
            pack(2, b, new[0:8])

    for place in range(3):
        for b in range(8):
            pack(place, b, a_ref[b % count, place * 8 : place * 8 + 8, :])
    u = panel(load(0), 0)
    n = advance(load(1), u)
    save(3, u)

    def turn(_, carry):
        n, before = carry[:8], carry[8:]
        q = [shift(x) for x in advance(load(2), before)]
        u = panel(n, 8)
        rest(3)
        n = advance(q, u)
        save(3, u)
        return tuple(n) + tuple(u)

    def turns(at, carry):
        for _ in range(3):
            carry = turn(at, carry)
        return carry

    carry = lax.fori_loop(0, (BLOCK // 8 - 1) // 3, turns, tuple(n) + tuple(u))
    rest(2)
    save(0, [shift(x) for x in carry[:8]])
    for b in range(count):
        a_ref[b, 0:8, :] = unpack(0, b)


def factor_kernel(f_ref, listed_ref, m_ref, n_ref, a_ref, hot, c11, c21, c22, w2, w3, *room):
    count = 4
    listed = listed_ref[0, 0]
    slot, within = listed >> 9, listed & 511
    third = (slot * 11) >> 5
    row = third * 2 + (within >> 8) - 1
    col = (slot - 3 * third) * 2 + ((within >> 7) & 1) - 1
    index = jnp.where(listed >= 0, (row * 4 + col) * BLOCK + (within & 127), -1)
    idx = index.astype(jnp.float32)
    idx = jnp.concatenate([idx, idx], axis=0)
    idx_t = idx.T
    lane = iota((1, BLOCK), 1).astype(jnp.float32)
    for b in range(count):
        chosen = idx_t[:, b : b + 1]
        for q, cell in enumerate(others(b)):
            same = chosen == lane + float(cell * BLOCK)
            hot[b, :, q * BLOCK : (q + 1) * BLOCK] = same.astype(jnp.float32).astype(jnp.bfloat16)
        near = jnp.concatenate(
            [f_ref[:, cell * BLOCK : (cell + 1) * BLOCK] for cell in others(b)], axis=1
        )
        stacked = jnp.concatenate([*thirds(near), jnp.zeros_like(near)], axis=0)
        found = pick(stacked.astype(jnp.bfloat16), hot[b], 1)
        x = found[0:8] + found[8:16] + found[16:24]
        xt = x.T
        live_row = (idx[b : b + 1, :] >= 0.0).astype(jnp.float32)
        live_col = (chosen >= 0.0).astype(jnp.float32)
        diagonal = live_row * x[3:4] + (1.0 - live_row)
        on_diagonal = iota((NEIGH, NEIGH), 0) == iota((NEIGH, NEIGH), 1)
        kern = kernel_value(xt[:, 0:1], xt[:, 1:2], xt[:, 2:3], x[0:1], x[1:2], x[2:3])
        c11[b] = kern * live_col * live_row + jnp.where(on_diagonal, diagonal, 0.0)
        home = OWN[b] * BLOCK
        o = f_ref[:, home : home + BLOCK]
        ot = o.T
        kern = kernel_value(ot[:, 0:1], ot[:, 1:2], ot[:, 2:3], x[0:1], x[1:2], x[2:3])
        c21[b] = kern * live_row
        on_diagonal = iota((BLOCK, BLOCK), 0) == iota((BLOCK, BLOCK), 1)
        kern = kernel_value(ot[:, 0:1], ot[:, 1:2], ot[:, 2:3], o[0:1], o[1:2], o[2:3])
        c22[b] = kern + jnp.where(on_diagonal, o[3:4], 0.0)
        a_ref[b] = c11[b, 0:BLOCK, 0:BLOCK]
    invert(a_ref, count, *room)
    for b in range(count):
        inverse = a_ref[b]
        a21 = c11[b, BLOCK:, 0:BLOCK]
        own1 = c21[b, :, 0:BLOCK]
        left2, left3 = dot(a21, inverse), dot(own1, inverse)
        w2[b], w3[b] = left2, left3
        a_ref[b] = c11[b, BLOCK:, BLOCK:] - dot(left2, a21, 1)
        c21[b, :, BLOCK:] = c21[b, :, BLOCK:] - dot(left3, a21, 1)
        c22[b] = c22[b] - dot(left3, own1, 1)
    invert(a_ref, count, *room)
    for b in range(count):
        own2 = c21[b, :, BLOCK:]
        b2 = dot(own2, a_ref[b])
        c21[b, :, 0:BLOCK] = dot(b2, w2[b]) - w3[b]
        a_ref[b] = c22[b] - dot(b2, own2, 1)
        c21[b, :, BLOCK:] = -b2
    invert(a_ref, count, *room)
    eye = (iota((BLOCK, BLOCK), 0) == iota((BLOCK, BLOCK), 1)).astype(jnp.float32)
    for b in range(count):
        inverse = a_ref[b]
        compact = c21[b]
        for ref, mine, theirs in ((m_ref, eye, compact), (n_ref, inverse, dot(inverse, compact))):
            stacked = jnp.concatenate(thirds(theirs), axis=0).astype(jnp.bfloat16)
            wide = pick(stacked, hot[b])
            wide = wide[0:BLOCK] + wide[BLOCK : 2 * BLOCK] + wide[2 * BLOCK :]
            ref[b, :, 0 : 4 * BLOCK] = wide[:, : 4 * BLOCK]
            ref[b, :, 4 * BLOCK : 5 * BLOCK] = mine
            ref[b, :, 5 * BLOCK :] = wide[:, 4 * BLOCK :]


def solve_kernel(nx, ny, f_ref, m_ref, n_ref, mean_ref, res_ref, k_ref, *scratch):
    (res, terms, terms_in, total, image, image_in, sums, sums_y, sums_x) = scratch[:9]
    (send_t, recv_t, send_i, recv_i, send_y, recv_y, send_x, recv_x) = scratch[9:]
    links = Links(nx, ny)
    gx, gy = links.x, links.y
    barrier = pltpu.get_barrier_semaphore()
    corners = links.greet(barrier, [k for k in range(8) if 0 not in DIRS[k]])
    line_y = [(gx, lax.rem(gy + off, ny)) for off in range(1, ny)]
    line_x = [(lax.rem(gx + off, nx), gy) for off in range(1, nx)]
    for peer in line_y + line_x:
        pl.semaphore_signal(barrier, inc=1, device_id=peer, device_id_type=MESH)
    for cell in range(16):
        res[cell : cell + 1, :] = f_ref[4:5, cell * BLOCK : (cell + 1) * BLOCK]
    noise = [f_ref[3:4, c * BLOCK : (c + 1) * BLOCK] for c in OWN]

    def precondition(step):
        out = [jnp.zeros((1, BLOCK), jnp.float32) for _ in range(16)]
        for b in range(4):
            acc = jnp.zeros((BLOCK, BLOCK), jnp.float32)
            for q, cell in enumerate(around(b)):
                acc = acc + m_ref[b, :, q * BLOCK : (q + 1) * BLOCK] * res[cell : cell + 1, :]
            w = jnp.sum(acc, axis=1, keepdims=True)
            for q, cell in enumerate(around(b)):
                part = n_ref[b, :, q * BLOCK : (q + 1) * BLOCK] * w
                out[cell] = out[cell] + jnp.sum(part, axis=0, keepdims=True)
        for cell in range(16):
            terms[step, cell : cell + 1, :] = out[cell]

    def fill_kernel():
        parts = [f_ref[:, cell * BLOCK : (cell + 1) * BLOCK] for cell in range(16)]
        turned = [part.T for part in parts]
        for b in range(4):
            o = parts[OWN[b]]
            for q, cell in enumerate(around(b)):
                t = turned[cell]
                kern = kernel_value(t[:, 0:1], t[:, 1:2], t[:, 2:3], o[0:1], o[1:2], o[2:3])
                k_ref[b, q * BLOCK : (q + 1) * BLOCK, :] = kern

    def exchange_terms(step):
        args = (terms.at[step], terms_in.at[step], send_t.at[step], recv_t.at[step])
        links.start(*args)
        if step == 0:
            fill_kernel()
        links.finish(*args)
        for cell in range(16):
            r, c = cell // 4, cell % 4
            value = terms[step, cell : cell + 1, :]
            for k, (dx, dy) in enumerate(DIRS):
                rr, cc = r - 2 * dx, c - 2 * dy
                if 0 <= rr < 4 and 0 <= cc < 4:
                    at = rr * 4 + cc
                    value = value + terms_in[step, k, at : at + 1, :]
            total[step, cell : cell + 1, :] = value

    def operate(step):
        columns = total[step].T
        for b in range(4):
            acc = jnp.zeros((BLOCK, BLOCK), jnp.float32)
            for q, cell in enumerate(around(b)):
                acc = acc + k_ref[b, q * BLOCK : (q + 1) * BLOCK, :] * columns[:, cell : cell + 1]
            value = jnp.sum(acc, axis=0, keepdims=True)
            value = value + noise[b] * total[step, OWN[b] : OWN[b] + 1, :]
            image[step, b : b + 1, :] = value

    def line_copy(step, buf, send, recv, peer, at, off):
        return pltpu.make_async_remote_copy(
            src_ref=sums.at[step, 0] if buf is sums_y else sums.at[step, 1],
            dst_ref=buf.at[step, at],
            send_sem=send.at[step, off],
            recv_sem=recv.at[step, off],
            device_id=peer,
            device_id_type=MESH,
        )

    def reduce_line(step, buf, send, recv, peers, me, size):
        copies = [line_copy(step, buf, send, recv, p, me, o) for o, p in enumerate(peers)]
        for copy in copies:
            copy.start()
        buf[step, me] = sums[step, 0] if buf is sums_y else sums[step, 1]
        for copy in copies:
            copy.wait()
        value = buf[step, 0]
        for at in range(1, size):
            value = value + buf[step, at]
        return value

    def reduce_all(step, *rows):
        sums[step, 0] = jnp.zeros((8, BLOCK), jnp.float32)
        for at, row in enumerate(rows):
            sums[step, 0, at : at + 1, :] = row
        sums[step, 1] = reduce_line(step, sums_y, send_y, recv_y, line_y, gy, ny)
        value = reduce_line(step, sums_x, send_x, recv_x, line_x, gx, nx)
        value = jnp.sum(value, axis=1, keepdims=True)
        return [value[at : at + 1, :] for at in range(len(rows))]

    def across(pairs):
        value = pairs[0][0] * pairs[0][1]
        for a, b in pairs[1:]:
            value = value + a * b
        return value

    def mine(ref, step):
        return [ref[step, c : c + 1, :] for c in OWN]

    precondition(0)
    pl.semaphore_wait(barrier, corners + nx + ny - 2)
    exchange_terms(0)
    image[...] = jnp.zeros_like(image)
    operate(0)
    args = (image.at[0], image_in, send_i, recv_i)
    links.start(*args)
    first = mine(total, 0)
    along = [image[0, b : b + 1, :] for b in range(4)]
    start = [res[c : c + 1, :] for c in OWN]
    current, curve = reduce_all(
        0, across(list(zip(start, first))), across(list(zip(first, along)))
    )
    links.finish(*args)
    alpha = current / curve
    for cell in range(16):
        way, inner = source_of(cell)
        if way == (0, 0):
            value = image[0, inner : inner + 1, :]
        else:
            value = image_in[DIRS.index(way), inner : inner + 1, :]
        res[cell : cell + 1, :] = res[cell : cell + 1, :] - alpha * value
    precondition(1)
    exchange_terms(1)
    operate(1)
    second = mine(total, 1)
    along2 = [image[1, b : b + 1, :] for b in range(4)]
    left = [res[c : c + 1, :] for c in OWN]
    following, own_curve, cross = reduce_all(
        1,
        across(list(zip(left, second))),
        across(list(zip(second, along2))),
        across(list(zip(second, along))),
    )
    ratio = following / current
    alpha2 = following / (own_curve + ratio * (2.0 * cross + ratio * curve))
    for b in range(4):
        solved = alpha * first[b] + alpha2 * (second[b] + ratio * first[b])
        mean_ref[b : b + 1, :] = start[b] - noise[b] * solved
        res_ref[b : b + 1, :] = left[b] - alpha2 * (along2[b] + ratio * along[b])


def local(nx, ny, coords, neighbours, noise_var, observations):
    tile = observations.shape[2]
    f32 = jnp.float32
    vmem = pl.BlockSpec(memory_space=pltpu.VMEM)
    dma = pltpu.SemaphoreType.DMA
    patch = pl.pallas_call(
        functools.partial(halo_kernel, nx, ny),
        out_shape=jax.ShapeDtypeStruct((8, 16 * BLOCK), f32),
        in_specs=[vmem] * 3,
        out_specs=vmem,
        scratch_shapes=[
            pltpu.VMEM((8, tile), f32),
            pltpu.VMEM((8, 8, tile), f32),
            dma((8,)),
            dma((8,)),
        ],
        compiler_params=pltpu.CompilerParams(collective_id=0, has_side_effects=True),
        name="halo",
    )(coords, noise_var.reshape(1, tile), observations.reshape(1, tile))
    wide = jax.ShapeDtypeStruct((4, BLOCK, 9 * BLOCK), f32)
    square = pltpu.VMEM((4, BLOCK, BLOCK), f32)
    m, n = pl.pallas_call(
        factor_kernel,
        out_shape=(wide, wide),
        in_specs=[vmem] * 2,
        out_specs=[vmem] * 2,
        scratch_shapes=[
            square,
            pltpu.VMEM((4, NEIGH, 8 * BLOCK), jnp.bfloat16),
            pltpu.VMEM((4, NEIGH, NEIGH), f32),
            pltpu.VMEM((4, BLOCK, NEIGH), f32),
            square,
            square,
            square,
            pltpu.VMEM((256, BLOCK), f32),
        ],
        compiler_params=pltpu.CompilerParams(vmem_limit_bytes=48 << 20),
        name="factor",
    )(patch, neighbours)
    mean, residual = pl.pallas_call(
        functools.partial(solve_kernel, nx, ny),
        out_shape=(jax.ShapeDtypeStruct((4, BLOCK), f32),) * 2,
        in_specs=[vmem] * 3,
        out_specs=[vmem] * 2,
        scratch_shapes=[
            pltpu.VMEM((4, 9 * BLOCK, BLOCK), f32),
            pltpu.VMEM((16, BLOCK), f32),
            pltpu.VMEM((2, 16, BLOCK), f32),
            pltpu.VMEM((2, 8, 16, BLOCK), f32),
            pltpu.VMEM((2, 16, BLOCK), f32),
            pltpu.VMEM((2, 8, BLOCK), f32),
            pltpu.VMEM((8, 8, BLOCK), f32),
            pltpu.VMEM((2, 2, 8, BLOCK), f32),
            pltpu.VMEM((2, ny, 8, BLOCK), f32),
            pltpu.VMEM((2, nx, 8, BLOCK), f32),
            dma((2, 8)),
            dma((2, 8)),
            dma((8,)),
            dma((8,)),
            dma((2, ny)),
            dma((2, ny)),
            dma((2, nx)),
            dma((2, nx)),
        ],
        compiler_params=pltpu.CompilerParams(
            collective_id=1, has_side_effects=True, vmem_limit_bytes=48 << 20
        ),
        name="solve",
    )(patch, m, n)
    return (mean.reshape(observations.shape), residual.reshape(observations.shape))


def solution(mesh):
    in_specs = (
        P(None, "gx", "gy", None),
        P("gx", "gy", None, None),
        P("gx", "gy", None),
        P("gx", "gy", None),
    )
    out_specs = (P("gx", "gy", None), P("gx", "gy", None))
    body = functools.partial(local, mesh.shape["gx"], mesh.shape["gy"])
    return jax.shard_map(body, mesh=mesh, in_specs=in_specs, out_specs=out_specs, check_vma=False)
```
